32 devices in a mesh: ctx: 16 (over z, x, core), dp: 2 (over y).
Axes of the slice: x: 2, y: 2, z: 4, core: 2. Of those that a mesh axis runs over, the one named last changes fastest.
Arguments:
- queries: bfloat16 [4096, 4096], P(None, ('ctx', 'dp')), may hold values from -6 to 6
- key_stream: bfloat16 [4096, 4096], P(None, ('ctx', 'dp')), may hold values from -6 to 6
- value_stream: bfloat16 [4096, 4096], P(None, ('ctx', 'dp')), may hold values from -6 to 6
- filters: float32 [256, 4096], P(('ctx', 'dp')), may hold values from -1 to 1
- bias: float32 [4096], P(('ctx', 'dp')), may hold values from -4 to 4
- grad_out: bfloat16 [4096, 4096], P(None, ('ctx', 'dp')), may hold values from -6 to 6
Outputs:
- out: bfloat16 [4096, 4096], P(None, ('ctx', 'dp'))
- grad_queries: bfloat16 [4096, 4096], P(None, ('ctx', 'dp'))
- grad_keys: bfloat16 [4096, 4096], P(None, ('ctx', 'dp'))
- grad_values: bfloat16 [4096, 4096], P(None, ('ctx', 'dp'))
- grad_filters: float32 [256, 4096], P(('ctx', 'dp'))
- grad_bias: float32 [4096], P(('ctx', 'dp'))
The draws below stay inside these ranges and needn't reach their ends.
All inputs are finite; a program needn't handle non-finite values.
Results may differ from the reference program's by a relative error of at most 0.006.
Values may be sent and summed in bfloat16 or wider, within the bound.
No kernel may reach another device: no remote copies, remote signals or barrier semaphores. Data moves between devices by JAX's collectives and lax.ppermute only.
A program may use at most 128 MiB of HBM per device.

```python
import math
import jax
import jax.numpy as jnp
from jax import lax

C = 4096
GROUP = 16
G = 256
SEQ = 4096


def draw_filters(key, part):
    noise = jnp.clip(jax.random.normal(key, (G, SEQ), jnp.float32), -6.0, 6.0)
    factor = 1.0 / math.sqrt(SEQ)
    return noise * factor


def shard_levels(own_key, extent, split, smallest, top_value):
    level = 1.0
    for dim, shards_of in split:
        heights = jax.random.uniform(jax.random.fold_in(jax.random.fold_in(own_key, 6), dim), (shards_of,), jnp.float32, smallest / len(split), top_value / len(split))
        level = level * jnp.repeat(jnp.exp(heights), extent[dim] // shards_of).reshape((-1,) + (1,) * (len(extent) - 1 - dim))
    return level


def centred(own_key, extent, scale, limit, shards=(), kind=jnp.bfloat16):
    drawn = jax.random.normal(own_key, extent, jnp.float32) * scale
    if len(shards) > 0:
        drawn = shard_levels(own_key, extent, shards, -0.22, 0.18) * drawn
    return jnp.clip(drawn, min=-limit, max=limit).astype(kind)


def setup_inputs(seed: int = 0) -> dict:
    streams_of = jax.random.split(jax.random.key(seed), 7)
    queries = centred(streams_of[0], (C, SEQ), 1.0, 6.0, ((1, 32),))
    key_stream = centred(streams_of[1], (C, SEQ), 1.0, 6.0, ((1, 32),))
    value_stream = centred(streams_of[2], (C, SEQ), 1.0, 6.0, ((1, 32),))
    filters = draw_filters(jax.random.fold_in(streams_of[6], 71), 0)
    bias = centred(streams_of[4], (C,), 1.0, 4.0, ((0, 32),), jnp.float32)
    grad_out = centred(streams_of[5], (C, SEQ), 1.0, 6.0, ((1, 32),))
    return dict(queries=queries, key_stream=key_stream, value_stream=value_stream, filters=filters, bias=bias, grad_out=grad_out)


def reference(queries, key_stream, value_stream, filters, bias, grad_out):
    product = (key_stream.astype(jnp.float32) * value_stream.astype(jnp.float32)).astype(jnp.bfloat16)
    weighted = (queries.astype(jnp.float32) * grad_out.astype(jnp.float32)).astype(jnp.bfloat16)
    length = 2 * SEQ

    def per_group(operands):
        taps, inputs, cotangent, offsets = operands
        inputs = inputs.astype(jnp.float32)
        cotangent = cotangent.astype(jnp.float32)
        taps_hat = jnp.fft.rfft(taps, n=length)
        inputs_hat = jnp.fft.rfft(inputs, n=length, axis=-1)
        cotan_hat = jnp.fft.rfft(cotangent, n=length, axis=-1)
        conv = jnp.fft.irfft(taps_hat[None, :] * inputs_hat, n=length, axis=-1)[:, :SEQ]
        corr = jnp.fft.irfft(jnp.conj(taps_hat)[None, :] * cotan_hat, n=length, axis=-1)[:, :SEQ]
        mixed = (conv + offsets[:, None] * inputs).astype(jnp.bfloat16)
        back = (corr + offsets[:, None] * cotangent).astype(jnp.bfloat16)
        lagged = jnp.fft.irfft(jnp.sum(cotan_hat * jnp.conj(inputs_hat), axis=0), n=length)[:SEQ]
        offset_grad = jnp.sum(cotangent * inputs, axis=1)
        return mixed, back, lagged, offset_grad

    mixed, back, lagged, offset_grad = lax.map(
        per_group,
        (filters, product.reshape(G, GROUP, SEQ), weighted.reshape(G, GROUP, SEQ), bias.reshape(G, GROUP)))
    mixed = mixed.reshape(C, SEQ).astype(jnp.float32)
    back = back.reshape(C, SEQ).astype(jnp.float32)
    out = (queries.astype(jnp.float32) * mixed).astype(jnp.bfloat16)
    grad_queries = (grad_out.astype(jnp.float32) * mixed).astype(jnp.bfloat16)
    grad_keys = (back * value_stream.astype(jnp.float32)).astype(jnp.bfloat16)
    grad_values = (back * key_stream.astype(jnp.float32)).astype(jnp.bfloat16)
    return out, grad_queries, grad_keys, grad_values, lagged.astype(jnp.float32), offset_grad.reshape(C).astype(jnp.float32)
```

```python
import functools

import jax
import jax.numpy as jnp
from jax import lax
from jax.experimental import pallas as pl
from jax.experimental.pallas import tpu as pltpu
from jax.sharding import Mesh, PartitionSpec as P

F32 = jnp.float32
BF16 = jnp.bfloat16
WIDTH = 128
WIDE = 2 * WIDTH
TIMES = (((1,), (0,)), ((), ()))
TIMES_T = (((1,), (1,)), ((), ()))
RING = ("ctx_low", "dp")
SPLIT_TAPS = True


def loop(count, body):
    if count <= 16:
        for step in range(count):
            body(step)
    else:
        lax.fori_loop(0, count, lambda step, none: (body(step), none)[1], 0)


def prepare_kernel(role, q, k, v, g, first, second, own):
    product = (k[...].astype(F32) * v[...].astype(F32)).astype(BF16)
    weighted = (q[...].astype(F32) * g[...].astype(F32)).astype(BF16)
    lead = role[0] == 0
    x = jnp.where(lead, product, weighted)
    y = jnp.where(lead, weighted, product)
    first[0] = x[0, 0]
    second[0] = x[1, 0]
    own[0] = y[:, 0]


def prepare(role, q, k, v, g, ranks):
    channels, tokens = q.shape
    per = channels // (2 * ranks)
    view = lambda a: a.reshape(2, ranks, per, tokens)
    spec = pl.BlockSpec((2, 1, per, tokens), lambda h, r: (0, h, 0, 0))
    half = jax.ShapeDtypeStruct((ranks, per, tokens), BF16)
    half_spec = pl.BlockSpec((1, per, tokens), lambda h, r: (h, 0, 0))
    return pl.pallas_call(
        prepare_kernel,
        out_shape=(half, half, jax.ShapeDtypeStruct((ranks, 2, per, tokens), BF16)),
        grid_spec=pltpu.PrefetchScalarGridSpec(
            num_scalar_prefetch=1,
            grid=(ranks,),
            in_specs=[spec] * 4,
            out_specs=(
                half_spec,
                half_spec,
                pl.BlockSpec((1, 2, per, tokens), lambda h, r: (h, 0, 0, 0)),
            ),
        ),
        name="prepare",
    )(role, view(q), view(k), view(v), view(g))


def finish_kernel(role, q, k, v, g, one, two_a, two_b, out, gq, gk, gv):
    lead = role[0] == 0
    for part, two in ((0, two_a), (1, two_b)):
        o1 = one[0, part].astype(F32)
        o2 = two[0].astype(F32)
        mixed = jnp.where(lead, o1, o2)
        back = jnp.where(lead, o2, o1)
        out[part, 0] = (q[part, 0].astype(F32) * mixed).astype(BF16)
        gq[part, 0] = (g[part, 0].astype(F32) * mixed).astype(BF16)
        gk[part, 0] = (back * v[part, 0].astype(F32)).astype(BF16)
        gv[part, 0] = (back * k[part, 0].astype(F32)).astype(BF16)


def finish(role, q, k, v, g, one, two_a, two_b, ranks):
    channels, tokens = q.shape
    per = channels // (2 * ranks)
    view = lambda a: a.reshape(2, ranks, per, tokens)
    spec = pl.BlockSpec((2, 1, per, tokens), lambda h, r: (0, h, 0, 0))
    half_spec = pl.BlockSpec((1, per, tokens), lambda h, r: (h, 0, 0))
    outs = pl.pallas_call(
        finish_kernel,
        out_shape=(jax.ShapeDtypeStruct((2, ranks, per, tokens), BF16),) * 4,
        grid_spec=pltpu.PrefetchScalarGridSpec(
            num_scalar_prefetch=1,
            grid=(ranks,),
            in_specs=[spec] * 4
            + [pl.BlockSpec((1, 2, per, tokens), lambda h, r: (h, 0, 0, 0)), half_spec, half_spec],
            out_specs=(spec,) * 4,
        ),
        name="finish",
    )(role, view(q), view(k), view(v), view(g), one, two_a, two_b)
    return [o.reshape(channels, tokens) for o in outs]


def build_tiles(role, taps, high, low, total, count):
    rows = lax.broadcasted_iota(jnp.int32, (WIDTH, WIDTH), 0)
    cols = lax.broadcasted_iota(jnp.int32, (WIDTH, WIDTH), 1)
    upper = cols >= rows
    zero = jnp.zeros((WIDTH, WIDTH), BF16)
    high[0] = zero
    if SPLIT_TAPS:
        low[0] = zero
    base = jnp.where(role == 0, 0, total - count)

    def skew(row):
        line = jnp.broadcast_to(taps[pl.ds(row, 1), :], (WIDTH, WIDTH))
        return pltpu.roll(line, 0, 1, stride=1, stride_axis=0)

    def step(t, before):
        row = base + t + 1
        here = skew(row)
        tile = jnp.where(upper, here, before)
        slot = jnp.where(role == 0, row, total - row + 1)
        top = tile.astype(BF16)
        high[slot] = top
        if SPLIT_TAPS:
            low[slot] = (tile - top.astype(F32)).astype(BF16)
        return here

    lax.fori_loop(0, count, step, skew(base), unroll=2)


def big(tiles, d):
    mid = tiles[2 * d + 1]
    return jnp.concatenate(
        [
            jnp.concatenate([mid, tiles[2 * d + 2]], axis=1),
            jnp.concatenate([tiles[2 * d], mid], axis=1),
        ],
        axis=0,
    )


def gather_rows(role, src, dst, start, blocks, group):
    for i in range(blocks):
        at = jnp.where(role == 0, i, blocks - 1 - i)
        dst[pl.ds(start + (i // 2) * group, group), pl.ds((i % 2) * WIDTH, WIDTH)] = src[at]


def scatter_rows(role, acc, dst, blocks, group):
    value = acc[...].astype(BF16)
    for i in range(blocks):
        at = jnp.where(role == 0, i, blocks - 1 - i)
        lo = (i // 2) * group
        c = (i % 2) * WIDTH
        dst[at] = value[lo : lo + group, c : c + WIDTH]


def dot(a, b, form):
    return lax.dot_general(a, b, form, preferred_element_type=F32)


def add_bias(acc, data, bias, pairs, group):
    line = jnp.concatenate([bias, bias], axis=1)
    shaped = data.astype(F32).reshape(pairs, group, WIDE) * line[None]
    acc[...] += shaped.reshape(pairs * group, WIDE)


def lead_kernel(blocks, group, total, role_ref, x_a, x_b, taps, bias, out, xs, acc, high, low):
    role = role_ref[0]
    pairs = blocks // 2
    rows = pairs * group
    xs[pl.ds(0, rows), :] = jnp.zeros((rows, WIDE), BF16)

    @pl.when(pl.program_id(0) == 0)
    def _():
        gather_rows(role, x_a, xs, rows, blocks, group)

    @pl.when(pl.program_id(0) == 1)
    def _():
        gather_rows(role, x_b, xs, rows, blocks, group)

    build_tiles(role, taps.at[0, 0], high, low, total, blocks)
    acc[...] = jnp.zeros_like(acc)

    def body(d):
        data = xs[pl.ds((pairs - d) * group, rows), :]
        add = dot(data, big(high, d), TIMES)
        if SPLIT_TAPS:
            add += dot(data, big(low, d), TIMES)
        acc[...] += add

    loop(pairs, body)
    add_bias(acc, xs[pl.ds(rows, rows), :], bias[0], pairs, group)
    scatter_rows(role, acc, out.at[:, 0], blocks, group)


def lead(role, x_a, x_b, taps, bias, group):
    blocks, per, tokens = x_a.shape
    groups = per // group
    total = taps.shape[2] - 1
    pairs = blocks // 2
    rows = pairs * group
    data_a = pl.BlockSpec((blocks, group, tokens), lambda p, i, r: (0, jnp.where(p == 0, i, groups - 1), 0))
    data_b = pl.BlockSpec((blocks, group, tokens), lambda p, i, r: (0, jnp.where(p == 1, i, 0), 0))
    return pl.pallas_call(
        functools.partial(lead_kernel, blocks, group, total),
        out_shape=jax.ShapeDtypeStruct((blocks, 2, per, tokens), BF16),
        grid_spec=pltpu.PrefetchScalarGridSpec(
            num_scalar_prefetch=1,
            grid=(2, groups),
            in_specs=[
                data_a,
                data_b,
                pl.BlockSpec((1, 1, total + 1, WIDTH), lambda p, i, r: (p, i, 0, 0)),
                pl.BlockSpec((1, group, WIDTH), lambda p, i, r: (p, i, 0)),
            ],
            out_specs=pl.BlockSpec((blocks, 1, group, tokens), lambda p, i, r: (0, p, i, 0)),
            scratch_shapes=[
                pltpu.VMEM((2 * rows, WIDE), BF16),
                pltpu.VMEM((rows, WIDE), F32),
                pltpu.VMEM((blocks + 1, WIDTH, WIDTH), BF16),
                pltpu.VMEM((blocks + 1, WIDTH, WIDTH), BF16),
            ],
        ),
        name="lead",
    )(role, x_a, x_b, taps, bias)


def follow_kernel(
    part, blocks, group, total, role_ref, x, y, r, taps, bias,
    out, dtaps, dbias, xs, ys, yg, acc, high, low, lines, keep,
):
    role = role_ref[0]
    pairs = blocks // 2
    rows = pairs * group
    own = role == part
    gather_rows(role, x, xs, 0, blocks, group)
    gather_rows(role, y.at[:, 0], ys, 0, blocks, group)
    gather_rows(role, r, ys, rows, blocks, group)
    zeros = jnp.zeros((rows, WIDE), BF16)
    ys[pl.ds(2 * rows, rows), :] = zeros
    yg[pl.ds(0, rows), :] = ys[pl.ds(0, rows), :]
    yg[pl.ds(rows, rows), :] = jnp.where(own, ys[pl.ds(rows, rows), :], zeros)
    yg[pl.ds(2 * rows, rows), :] = zeros
    build_tiles(role, taps.at[0, 0], high, low, total, total)
    acc[...] = jnp.zeros_like(acc)

    def body(d):
        data = ys[pl.ds(d * group, rows), :]
        add = dot(data, big(high, d), TIMES_T)
        if SPLIT_TAPS:
            add += dot(data, big(low, d), TIMES_T)
        acc[...] += add

    loop(2 * pairs, body)
    mine = ys[pl.ds(0, rows), :]
    add_bias(acc, mine, bias[0], pairs, group)
    scatter_rows(role, acc, out, blocks, group)

    both = xs[...].astype(F32) * mine.astype(F32)
    both = jnp.sum(both.reshape(pairs, group, WIDE), axis=0)
    dbias[...] = both[:, :WIDTH] + both[:, WIDTH:]

    lines[...] = jnp.zeros_like(lines)
    down = lax.broadcasted_iota(jnp.int32, (WIDE, WIDE), 0)
    across = lax.broadcasted_iota(jnp.int32, (WIDE, WIDE), 1)
    mirror = jnp.where(down < WIDTH, WIDTH - 1 - down, WIDE + WIDTH - 1 - down)
    mirror = jnp.where(across == mirror, 1.0, 0.0).astype(BF16)
    turned = dot(mirror, xs[...], TIMES_T).astype(BF16)
    inside = lax.broadcasted_iota(jnp.int32, (WIDTH, WIDTH), 1) <= lax.broadcasted_iota(
        jnp.int32, (WIDTH, WIDTH), 0
    )

    def unskew(square, lag):
        flat = pltpu.roll(square, 1, 1, stride=1, stride_axis=0)
        kept = jnp.where(inside, flat, 0.0)
        rest = flat - kept
        at = jnp.where(role == 0, lag + 1, total - lag)
        lines[at] += jnp.sum(kept.reshape(WIDTH // 8, 8, WIDTH), axis=0)
        lines[at - 1] += jnp.sum(rest.reshape(WIDTH // 8, 8, WIDTH), axis=0)

    keep[...] = jnp.zeros_like(keep)

    def grad(d):
        square = dot(turned, yg[pl.ds(d * group, rows), :], TIMES)
        unskew(square[:WIDTH, :WIDTH] + square[WIDTH:, WIDTH:], 2 * d)
        cross = keep[...] + square[WIDTH:, :WIDTH]

        if isinstance(d, int):
            if d > 0:
                unskew(cross, 2 * d - 1)
        else:
            @pl.when(d > 0)
            def _():
                unskew(cross, 2 * d - 1)

        keep[...] = square[:WIDTH, WIDTH:]

    loop(pairs, grad)

    @pl.when(own)
    def _():
        if pairs <= 16:
            for d in range(pairs, 2 * pairs):
                grad(d)
        else:
            lax.fori_loop(pairs, 2 * pairs, lambda d, none: (grad(d), none)[1], 0)
        unskew(keep[...], 4 * pairs - 1)

    @pl.when(jnp.logical_not(own))
    def _():
        unskew(keep[...], 2 * pairs - 1)

    dtaps[0] = jnp.sum(lines[...], axis=1)


def follow(part, role, x, y, r, taps, bias, group):
    blocks, per, tokens = x.shape
    groups = per // group
    total = taps.shape[2] - 1
    pairs = blocks // 2
    rows = pairs * group
    data = pl.BlockSpec((blocks, group, tokens), lambda i, s: (0, i, 0))
    return pl.pallas_call(
        functools.partial(follow_kernel, part, blocks, group, total),
        out_shape=(
            jax.ShapeDtypeStruct((blocks, per, tokens), BF16),
            jax.ShapeDtypeStruct((groups, total + 1, WIDTH), F32),
            jax.ShapeDtypeStruct((per, WIDTH), F32),
        ),
        grid_spec=pltpu.PrefetchScalarGridSpec(
            num_scalar_prefetch=1,
            grid=(groups,),
            in_specs=[
                data,
                pl.BlockSpec((blocks, 1, group, tokens), lambda i, s: (0, part, i, 0)),
                data,
                pl.BlockSpec((1, 1, total + 1, WIDTH), lambda i, s: (part, i, 0, 0)),
                pl.BlockSpec((1, group, WIDTH), lambda i, s: (part, i, 0)),
            ],
            out_specs=(
                data,
                pl.BlockSpec((1, total + 1, WIDTH), lambda i, s: (i, 0, 0)),
                pl.BlockSpec((group, WIDTH), lambda i, s: (i, 0)),
            ),
            scratch_shapes=[
                pltpu.VMEM((rows, WIDE), BF16),
                pltpu.VMEM((3 * rows, WIDE), BF16),
                pltpu.VMEM((3 * rows, WIDE), BF16),
                pltpu.VMEM((rows, WIDE), F32),
                pltpu.VMEM((total + 1, WIDTH, WIDTH), BF16),
                pltpu.VMEM((total + 1, WIDTH, WIDTH), BF16),
                pltpu.VMEM((total + 1, 8, WIDTH), F32),
                pltpu.VMEM((WIDTH, WIDTH), F32),
            ],
        ),
        name="follow",
    )(role, x, y, r, taps, bias)


def exchange(values):
    return lax.all_to_all(values, RING, split_axis=0, concat_axis=0)


def local(queries, key_stream, value_stream, filters, bias, grad_out):
    ranks = lax.axis_size(RING)
    half = lax.axis_index("half")
    role = half.astype(jnp.int32)[None]
    groups, length = filters.shape
    total = length // WIDTH
    group = bias.shape[0] // groups
    partner = [(i, (i + ranks) % (2 * ranks)) for i in range(2 * ranks)]
    everyone = ("half",) + RING
    swap = lambda a: lax.ppermute(a, everyone, partner)
    order = lambda mine, other: jnp.where(half == 0, jnp.stack([mine, other]), jnp.stack([other, mine]))

    x_a, x_b, y = prepare(role, queries, key_stream, value_stream, grad_out, ranks)
    x_a = exchange(x_a)
    x_b = exchange(x_b)
    packed = jnp.concatenate([filters, jnp.pad(bias.reshape(groups, group), ((0, 0), (0, WIDTH - group)))], axis=1)
    other = swap(packed)
    taps = order(packed[:, :length], other[:, :length])
    offsets = order(bias, other[:, length : length + group].reshape(-1))
    ahead = jnp.pad(taps, ((0, 0), (0, 0), (WIDTH, 0)))
    behind = jnp.pad(jnp.flip(taps, axis=2), ((0, 0), (0, 0), (1, WIDTH - 1)))
    taps = jnp.where(half == 0, ahead, behind).reshape(2, groups, total + 1, WIDTH)
    offsets = jnp.broadcast_to(offsets[:, :, None], (2, groups * group, WIDTH))

    r_a = swap(x_a)
    r_b = swap(x_b)
    y = exchange(y)
    one = exchange(lead(role, x_a, x_b, taps, offsets, group))
    two_a, dt_a, db_a = follow(0, role, x_a, y, r_a, taps, offsets, group)
    two_a = exchange(two_a)
    two_b, dt_b, db_b = follow(1, role, x_b, y, r_b, taps, offsets, group)
    two_b = exchange(two_b)

    dtaps = jnp.stack([dt_a, dt_b]).reshape(2, groups, -1)
    dtaps = jnp.where(
        half == 0, dtaps[:, :, WIDTH:], jnp.flip(dtaps[:, :, 1 : length + 1], axis=2)
    )
    dbias = jnp.sum(jnp.stack([db_a, db_b]), axis=2)
    mine = lambda a: lax.dynamic_index_in_dim(a, half, 0, keepdims=False)
    rest = lambda a: lax.dynamic_index_in_dim(a, 1 - half, 0, keepdims=False)
    sent = jnp.concatenate(
        [
            rest(dtaps)[:, : length // 2],
            jnp.pad(rest(dbias).reshape(groups, group), ((0, 0), (0, WIDTH - group))),
        ],
        axis=1,
    )
    came = swap(sent)
    grad_filters = mine(dtaps) + jnp.pad(came[:, : length // 2], ((0, 0), (0, length // 2)))
    grad_bias = mine(dbias) + came[:, length // 2 : length // 2 + group].reshape(-1)
    outs = finish(role, queries, key_stream, value_stream, grad_out, one, two_a, two_b, ranks)
    return (*outs, grad_filters, grad_bias)


def solution(mesh):
    ctx, dp = mesh.devices.shape
    split = Mesh(mesh.devices.reshape(2, ctx // 2, dp), ("half", "ctx_low", "dp"))
    axes = ("half", "ctx_low", "dp")
    stream = P(None, axes)
    return jax.shard_map(
        local,
        mesh=split,
        in_specs=(stream, stream, stream, P(axes, None), P(axes), stream),
        out_specs=(stream, stream, stream, stream, P(axes, None), P(axes)),
        check_vma=False,
    )
```

```python
import functools

import jax
import jax.numpy as jnp
from jax import lax
from jax.experimental import pallas as pl
from jax.experimental.pallas import tpu as pltpu
from jax.sharding import Mesh, PartitionSpec as P


F32 = jnp.float32
BF16 = jnp.bfloat16
WIDTH = 128
WIDE = 2 * WIDTH
TIMES = (((1,), (0,)), ((), ()))
TIMES_T = (((1,), (1,)), ((), ()))
RING = ("ctx_low", "dp")
TAP_PARTS = 2
STEPS = 2
MANY = 4
SWEEP = 2
UNROLL = 16


def pick(role, cases):
    for case in (0, 1):
        pl.when(role == case)(functools.partial(cases, case))


def prepare_kernel(role, q, k, v, g, first, second, own):
    def main(case):
        product = (k[...].astype(F32) * v[...].astype(F32)).astype(BF16)
        weighted = (q[...].astype(F32) * g[...].astype(F32)).astype(BF16)
        x, y = (product, weighted) if case == 0 else (weighted, product)
        first[...] = x[0]
        second[...] = x[1]
        own[:, 0] = y[0]
        own[:, 1] = y[1]

    pick(role[0], main)


def prepare(role, q, k, v, g, ranks):
    channels, tokens = q.shape
    per = channels // (2 * ranks)
    view = lambda a: a.reshape(2, ranks, per, tokens)
    step = ranks // STEPS
    spec = pl.BlockSpec((2, step, per, tokens), lambda h, r: (0, h, 0, 0))
    half = jax.ShapeDtypeStruct((ranks, per, tokens), BF16)
    half_spec = pl.BlockSpec((step, per, tokens), lambda h, r: (h, 0, 0))
    return pl.pallas_call(
        prepare_kernel,
        out_shape=(half, half, jax.ShapeDtypeStruct((ranks, 2, per, tokens), BF16)),
        grid_spec=pltpu.PrefetchScalarGridSpec(
            num_scalar_prefetch=1,
            grid=(STEPS,),
            in_specs=[spec] * 4,
            out_specs=(
                half_spec,
                half_spec,
                pl.BlockSpec((step, 2, per, tokens), lambda h, r: (h, 0, 0, 0)),
            ),
        ),
        name="prepare",
    )(role, view(q), view(k), view(v), view(g))


def finish_kernel(role, q, k, v, g, one, two_a, two_b, out, gq, gk, gv):
    def main(case):
        for part, two in ((0, two_a), (1, two_b)):
            first, second = one[:, part].astype(F32), two[...].astype(F32)
            mixed, back = (first, second) if case == 0 else (second, first)
            out[part] = (q[part].astype(F32) * mixed).astype(BF16)
            gq[part] = (g[part].astype(F32) * mixed).astype(BF16)
            gk[part] = (back * v[part].astype(F32)).astype(BF16)
            gv[part] = (back * k[part].astype(F32)).astype(BF16)

    pick(role[0], main)


def finish(role, q, k, v, g, one, two_a, two_b, ranks):
    channels, tokens = q.shape
    per = channels // (2 * ranks)
    view = lambda a: a.reshape(2, ranks, per, tokens)
    step = ranks // STEPS
    spec = pl.BlockSpec((2, step, per, tokens), lambda h, r: (0, h, 0, 0))
    half_spec = pl.BlockSpec((step, per, tokens), lambda h, r: (h, 0, 0))
    outs = pl.pallas_call(
        finish_kernel,
        out_shape=(jax.ShapeDtypeStruct((2, ranks, per, tokens), BF16),) * 4,
        grid_spec=pltpu.PrefetchScalarGridSpec(
            num_scalar_prefetch=1,
            grid=(STEPS,),
            in_specs=[spec] * 4
            + [pl.BlockSpec((step, 2, per, tokens), lambda h, r: (h, 0, 0, 0)), half_spec, half_spec],
            out_specs=(spec,) * 4,
        ),
        name="finish",
    )(role, view(q), view(k), view(v), view(g), one, two_a, two_b)
    return [o.reshape(channels, tokens) for o in outs]


def sweep(count, body):
    lax.fori_loop(0, count, lambda n, none: (body(n), none)[1], 0, unroll=min(count, SWEEP))


def build_band(line_of, tiles, case, lags):
    total = tiles[0].shape[1] // WIDTH - 1
    first = 0 if case == 0 else total - lags
    chunk = min(lags, 32)

    def step(c):
        c = c * chunk + first
        if isinstance(c, int):
            line = line_of(slice(c * WIDTH, (c + chunk + 1) * WIDTH))
        else:
            line = line_of(pl.ds(pl.multiple_of(c * WIDTH, WIDTH), (chunk + 1) * WIDTH))
        line = jnp.broadcast_to(line, (WIDTH, (chunk + 1) * WIDTH))
        band = pltpu.roll(line, 0, 1, stride=1, stride_axis=0)[:, WIDTH:]
        place = pl.ds(pl.multiple_of((c + 1) * WIDTH, WIDTH), chunk * WIDTH)
        top = band.astype(BF16)
        tiles[0][:, place] = top
        if len(tiles) > 1:
            tiles[1][:, place] = (band - top.astype(F32)).astype(BF16)

    if lags == chunk:
        step(0)
    else:
        lax.fori_loop(0, lags // chunk, lambda c, none: (step(c), none)[1], 0)


def square_of(tiles, case, d, turned):
    total = tiles.shape[1] // WIDTH - 1

    def tile(lag):
        if isinstance(d, int) and lag < 0:
            return jnp.zeros((WIDTH, WIDTH), BF16)
        at = lag + 1 if case == 0 else total - lag
        if isinstance(d, int):
            return tiles[:, at * WIDTH : (at + 1) * WIDTH]
        value = tiles[:, pl.ds(pl.multiple_of(jnp.clip(at, 0, total) * WIDTH, WIDTH), WIDTH)]
        return jnp.where(lag < 0, jnp.zeros_like(value), value)

    mid, less, more = tile(2 * d), tile(2 * d - 1), tile(2 * d + 1)
    if turned:
        less, more = more, less
    return jnp.concatenate(
        [jnp.concatenate([mid, more], axis=1), jnp.concatenate([less, mid], axis=1)], axis=0
    )


def dot(a, b, form=TIMES):
    return lax.dot_general(a, b, form, preferred_element_type=F32)


def gather_rows(case, src, dst, start, blocks, group):
    for i in range(blocks):
        at = i if case == 0 else blocks - 1 - i
        row = start + (i // 2) * group
        col = (i % 2) * WIDTH
        dst[row : row + group, col : col + WIDTH] = src[at]


def scatter_rows(case, value, dst, blocks, group):
    for i in range(blocks):
        at = i if case == 0 else blocks - 1 - i
        row = (i // 2) * group
        col = (i % 2) * WIDTH
        dst[at] = value[row : row + group, col : col + WIDTH].astype(BF16)


def apply_band(data, start, sign, shift, lags, tiles, case, turned, acc, group, base=None):
    rows = acc.shape[0]
    pairs = rows // group
    if pairs <= UNROLL:
        sums = [None] * pairs
        if base is not None:
            sums = [base[i * group : (i + 1) * group, :] for i in range(pairs)]
        for d in range(*lags):
            at = [i for i in range(pairs) if 0 <= i + sign * d + shift < pairs]
            low = start + (at[0] + sign * d + shift) * group
            block = data[low : low + len(at) * group, :]
            for part in tiles:
                found = dot(block, square_of(part, case, d, turned))
                for k, i in enumerate(at):
                    piece = found[k * group : (k + 1) * group]
                    sums[i] = piece if sums[i] is None else sums[i] + piece
        return jnp.concatenate(sums, axis=0)
    acc[...] = jnp.zeros_like(acc) if base is None else base[...]

    def step(d, none):
        low = pl.multiple_of(start + (sign * d + shift) * group, group)
        block = data[pl.ds(low, rows), :]
        for part in tiles:
            acc[...] += dot(block, square_of(part, case, d, turned))
        return none

    lax.fori_loop(*lags, step, 0)
    return acc[...]


def bias_term(data, bias, pairs, group):
    line = jnp.concatenate([bias, bias], axis=1)
    shaped = data.astype(F32).reshape(pairs, group, WIDE) * line[None]
    return shaped.reshape(pairs * group, WIDE)


def flip_rows(data):
    down = lax.broadcasted_iota(jnp.int32, (WIDE, WIDE), 0)
    across = lax.broadcasted_iota(jnp.int32, (WIDE, WIDE), 1)
    mirror = jnp.where(down < WIDTH, WIDTH - 1 - down, WIDE + WIDTH - 1 - down)
    mirror = jnp.where(across == mirror, 1.0, 0.0).astype(BF16)
    return dot(mirror, data, TIMES_T).astype(BF16)


def correlate(case, turned, data, start, shift, lags, total, lines, group):
    rows = turned.shape[1]
    pairs = rows // group
    inside = lax.broadcasted_iota(jnp.int32, (WIDTH, WIDTH), 1) <= lax.broadcasted_iota(
        jnp.int32, (WIDTH, WIDTH), 0
    )

    def unskew(square, lag):
        flat = pltpu.roll(square, 1, 1, stride=1, stride_axis=0)
        kept = jnp.where(inside, flat, 0.0)
        at = lag + 1 if case == 0 else total - lag
        kept = jnp.sum(kept.reshape(WIDTH // 8, 8, WIDTH), axis=0)
        lines[at] += kept
        lines[at - 1] += jnp.sum(flat.reshape(WIDTH // 8, 8, WIDTH), axis=0) - kept

    def outer(d):
        low = start + (d + shift) * group
        if not isinstance(d, int):
            low = pl.multiple_of(low, group)
        return dot(turned, data[pl.ds(low, rows), :])

    first, last = lags
    if pairs <= UNROLL:
        keep = None
        for d in range(first, last):
            square = outer(d)
            unskew(square[:WIDTH, :WIDTH] + square[WIDTH:, WIDTH:], 2 * d)
            if d > 0:
                below = square[WIDTH:, :WIDTH]
                unskew(below if keep is None else keep + below, 2 * d - 1)
            keep = square[:WIDTH, WIDTH:]
    else:

        def step(d, keep):
            square = outer(d)
            unskew(square[:WIDTH, :WIDTH] + square[WIDTH:, WIDTH:], 2 * d)
            pl.when(d > 0)(lambda: unskew(keep + square[WIDTH:, :WIDTH], 2 * d - 1))
            return square[:WIDTH, WIDTH:]

        keep = lax.fori_loop(first, last, step, jnp.zeros((WIDTH, WIDTH), F32))
    unskew(keep, 2 * last - 1)


def fold_lines(lines, dtaps, row):
    here = lax.broadcasted_iota(jnp.int32, (dtaps.shape[0], WIDTH), 0) == row
    for j in range(lines.shape[0]):
        lanes = slice(j * WIDTH, (j + 1) * WIDTH)
        total = jnp.broadcast_to(jnp.sum(lines[j], axis=0, keepdims=True), here.shape)
        dtaps[:, lanes] = jnp.where(here, total, dtaps[:, lanes])


def row_of(taps, many, n):
    row = pl.program_id(0) * many + n
    return lambda lanes: taps[pl.ds(row, 1), lanes]


def lead_kernel(blocks, group, many, role, x, taps, bias, *rest):
    out, xs, acc, *tiles = rest[-3 - TAP_PARTS :]
    pairs = blocks // 2
    rows = pairs * group

    def each(case, n):
        place = pl.ds(pl.multiple_of(n * group, group), group)
        line, band = xs, tiles
        line[0:rows, :] = jnp.zeros((rows, WIDE), BF16)
        gather_rows(case, x.at[:, place], line, rows, blocks, group)
        build_band(row_of(taps, many, n), band, case, blocks)
        value = apply_band(line, rows, -1, 0, (0, pairs), band, case, False, acc, group)
        value += bias_term(line[rows : 2 * rows, :], bias[place], pairs, group)
        scatter_rows(case, value, out.at[:, place], blocks, group)

    pick(role[0], lambda case: sweep(many, functools.partial(each, case)))


def local_kernel(
    blocks, group, many, role, x, y, taps, bias, out, dtaps, dbias, xs, ys, acc, lines, *tiles
):
    pairs = blocks // 2
    rows = pairs * group

    def each(case, n):
        place = pl.ds(pl.multiple_of(n * group, group), group)
        lead, line, band = xs, ys, tiles
        line[rows : 2 * rows, :] = jnp.zeros((rows, WIDE), BF16)
        gather_rows(case, x.at[:, place], lead, 0, blocks, group)
        gather_rows(case, y.at[:, place], line, 0, blocks, group)
        build_band(row_of(taps, many, n), band, 1 - case, blocks)
        value = apply_band(line, 0, 1, 0, (0, pairs), band, 1 - case, True, acc, group)
        mine = line[0:rows, :]
        out[n] = value + bias_term(mine, bias[place], pairs, group)
        both = lead[...].astype(F32) * mine.astype(F32)
        both = jnp.sum(both.reshape(pairs, group, WIDE), axis=0)
        dbias[place] = both[:, :WIDTH] + both[:, WIDTH:]
        found = lines
        found[...] = jnp.zeros_like(found)
        correlate(case, flip_rows(lead[...]), line, 0, 0, (0, pairs), 2 * blocks, found, group)
        fold_lines(found, dtaps, pl.program_id(0) * many + n)

    pick(role[0], lambda case: sweep(many, functools.partial(each, case)))


def cross_kernel(blocks, group, many, role, r, taps, base, out, rs, acc, *tiles):
    pairs = blocks // 2
    rows = pairs * group

    def each(case, n):
        place = pl.ds(pl.multiple_of(n * group, group), group)
        line, band = rs, tiles
        zeros = jnp.zeros((rows, WIDE), BF16)
        line[0:rows, :] = zeros
        line[2 * rows : 3 * rows, :] = zeros
        gather_rows(case, r.at[:, place], line, rows, blocks, group)
        build_band(row_of(taps, many, n), band, 1 - case, 2 * blocks)
        value = apply_band(
            line, rows, 1, -pairs, (1, 2 * pairs), band, 1 - case, True, acc, group, base.at[n]
        )
        scatter_rows(case, value, out.at[:, place], blocks, group)

    pick(role[0], lambda case: sweep(many, functools.partial(each, case)))


def remote_kernel(blocks, group, many, role, x_a, x_b, r_a, r_b, dtaps, xs, rs, lines):
    pairs = blocks // 2
    rows = pairs * group

    def each(case, n):
        place = pl.ds(pl.multiple_of(n * group, group), group)
        x, r = (x_a, r_a) if case == 0 else (x_b, r_b)
        lead, line, found = xs, rs, lines
        zeros = jnp.zeros((rows, WIDE), BF16)
        line[0:rows, :] = zeros
        line[2 * rows : 3 * rows, :] = zeros
        gather_rows(case, x.at[:, place], lead, 0, blocks, group)
        gather_rows(case, r.at[:, place], line, rows, blocks, group)
        found[...] = jnp.zeros_like(found)
        correlate(
            case, flip_rows(lead[...]), line, rows, -pairs, (1, 2 * pairs), 2 * blocks, found, group
        )
        fold_lines(found, dtaps, pl.program_id(0) * many + n)

    pick(role[0], lambda case: sweep(many, functools.partial(each, case)))


class Sizes:
    def __init__(self, x, taps, group):
        self.group = group
        self.blocks, self.per, self.tokens = x.shape
        self.groups, self.width = taps.shape[1:]
        self.many = min(self.groups, MANY)
        self.rows = self.blocks // 2 * group
        self.data = pl.BlockSpec(
            (self.blocks, self.many * group, self.tokens), lambda i, s: (0, i, 0)
        )
        self.bands = [pltpu.VMEM((WIDTH, self.width), BF16)] * TAP_PARTS
        self.acc = pltpu.VMEM((self.rows, WIDE), F32)
        self.lines = pltpu.VMEM((self.width // WIDTH, 8, WIDTH), F32)
        self.stream = jax.ShapeDtypeStruct(x.shape, BF16)
        self.sums = jax.ShapeDtypeStruct((self.groups, self.rows, WIDE), F32)
        self.sums_spec = pl.BlockSpec((self.many, self.rows, WIDE), lambda i, s: (i, 0, 0))
        self.dtaps = jax.ShapeDtypeStruct((self.groups, self.width), F32)
        self.dtaps_spec = pl.BlockSpec((self.groups, self.width), lambda i, s: (0, 0))

    def held(self, count):
        return pltpu.VMEM((count * self.rows, WIDE), BF16)

    def taps(self, part):
        return pl.BlockSpec((None, self.groups, self.width), lambda i, s: (part, 0, 0))

    def bias(self, part):
        return pl.BlockSpec((None, self.many * self.group, WIDTH), lambda i, s: (part, i, 0))

    def call(self, kernel, out_shape, in_specs, out_specs, scratch, flops, aliases={}):
        return pl.pallas_call(
            functools.partial(kernel, self.blocks, self.group, self.many),
            out_shape=out_shape,
            grid_spec=pltpu.PrefetchScalarGridSpec(
                num_scalar_prefetch=1,
                grid=(self.groups // self.many,),
                in_specs=in_specs,
                out_specs=out_specs,
                scratch_shapes=scratch,
            ),
            cost_estimate=pl.CostEstimate(
                flops=flops, bytes_accessed=8 * self.blocks * self.per * self.tokens, transcendentals=0
            ),
            input_output_aliases=aliases,
        )

    def work(self, share):
        return int(share * 4 * self.groups * self.group * (self.blocks * self.tokens) ** 2)


def lead(part, role, x, taps, bias, group, before=None):
    z = Sizes(x, taps, group)
    out = jax.ShapeDtypeStruct((z.blocks, 2, z.per, z.tokens), BF16)
    spec = pl.BlockSpec(
        (z.blocks, None, z.many * group, z.tokens), lambda i, s: (0, part, i, 0)
    )
    more = [] if before is None else [before]
    return z.call(
        lead_kernel, out,
        [z.data, z.taps(part), z.bias(part)] + [pl.BlockSpec(memory_space=pl.ANY)] * len(more),
        spec, [z.held(2), z.acc] + z.bands, z.work(1), {} if before is None else {4: 0},
    )(role, x, taps, bias, *more)


def local_part(part, role, x, y, taps, bias, group):
    z = Sizes(x, taps, group)
    y_spec = pl.BlockSpec(
        (z.blocks, None, z.many * group, z.tokens), lambda i, s: (0, part, i, 0)
    )
    return z.call(
        local_kernel,
        (z.sums, z.dtaps, jax.ShapeDtypeStruct((z.per, WIDTH), F32)),
        [z.data, y_spec, z.taps(part), z.bias(part)],
        (z.sums_spec, z.dtaps_spec, pl.BlockSpec((z.many * group, WIDTH), lambda i, s: (i, 0))),
        [z.held(1), z.held(2), z.acc, z.lines] + z.bands, z.work(1.5),
    )(role, x, y, taps, bias)


def cross_part(part, role, r, taps, base, group):
    z = Sizes(r, taps, group)
    return z.call(
        cross_kernel, z.stream, [z.data, z.taps(part), z.sums_spec], z.data,
        [z.held(3), z.acc] + z.bands, z.work(2),
    )(role, r, taps, base)


def remote_part(role, x_a, x_b, r_a, r_b, taps, group):
    z = Sizes(x_a, taps, group)
    return z.call(
        remote_kernel, z.dtaps, [z.data] * 4, z.dtaps_spec,
        [z.held(1), z.held(3), z.lines], z.work(1),
    )(role, x_a, x_b, r_a, r_b)


def exact_parts(data):
    high = data.astype(BF16)
    rest = data - high.astype(F32)
    middle = rest.astype(BF16)
    return high, middle, (rest - middle.astype(F32)).astype(BF16)


def reverse_line(data, length, count):
    rows, width = data.shape
    total = length // WIDTH
    down = lax.broadcasted_iota(jnp.int32, (WIDTH, WIDTH), 0)
    across = lax.broadcasted_iota(jnp.int32, (WIDTH, WIDTH), 1)
    inner = jnp.where(down + across == WIDTH, 1.0, 0.0).astype(BF16)
    edge = jnp.where(down + across == 0, 1.0, 0.0).astype(BF16)
    zero = jnp.zeros((rows, WIDTH), F32)

    def block(t):
        return data[:, t * WIDTH : (t + 1) * WIDTH] if 0 <= t < width // WIDTH else zero

    done = []
    for j in range(count // WIDTH):
        found = zero
        for a, b in zip(exact_parts(block(total - 1 - j)), exact_parts(block(total - j))):
            found += dot(a, inner) + dot(b, edge)
        done.append(found)
    return jnp.concatenate(done, axis=1)


def arrange_kernel(role, mine, other, lead_taps, follow_taps, bias):
    groups, width = mine.shape
    length = width - WIDTH

    def main(case):
        for part in (0, 1):
            src = mine if part == case else other
            taps = src[:, :length]
            ahead = jnp.concatenate([jnp.zeros((groups, WIDTH), F32), taps], axis=1)
            behind = reverse_line(taps, length, width)
            first, second = (ahead, behind) if case == 0 else (behind, ahead)
            lead_taps[part] = first
            follow_taps[part] = second
            line = jnp.broadcast_to(src[0:1, length:], (WIDTH, WIDTH))
            bias[part] = line.T[: bias.shape[1]]

    pick(role[0], main)


def arrange(role, mine, other, per):
    groups, width = mine.shape
    taps = jax.ShapeDtypeStruct((2, groups, width), F32)
    return pl.pallas_call(
        arrange_kernel,
        out_shape=(taps, taps, jax.ShapeDtypeStruct((2, per, WIDTH), F32)),
        grid_spec=pltpu.PrefetchScalarGridSpec(
            num_scalar_prefetch=1,
            grid=(1,),
            in_specs=[pl.BlockSpec((groups, width), lambda i, s: (0, 0))] * 2,
            out_specs=(
                pl.BlockSpec((2, groups, width), lambda i, s: (0, 0, 0)),
                pl.BlockSpec((2, groups, width), lambda i, s: (0, 0, 0)),
                pl.BlockSpec((2, per, WIDTH), lambda i, s: (0, 0, 0)),
            ),
        ),
        name="arrange",
    )(role, mine, other)


def natural(case, dtaps, count):
    if case == 0:
        return dtaps[:, WIDTH : WIDTH + count]
    return reverse_line(dtaps, dtaps.shape[1] - WIDTH, count)


def channel_line(dbias):
    square = dbias[...]
    if square.shape[0] < WIDTH:
        square = jnp.concatenate(
            [square, jnp.zeros((WIDTH - square.shape[0], WIDTH), F32)], axis=0
        )
    return jnp.sum(square.T, axis=0, keepdims=True)


def send_kernel(role, dt_a, dt_b, db_a, db_b, sent):
    groups, width = dt_a.shape
    half = (width - WIDTH) // 2

    def main(case):
        taps, bias = (dt_b, db_b) if case == 0 else (dt_a, db_a)
        sent[:, :half] = natural(case, taps[...], half)
        sent[:, half:] = jnp.broadcast_to(channel_line(bias), (groups, WIDTH))

    pick(role[0], main)


def receive_kernel(role, dt_a, dt_b, db_a, db_b, far, came, grad_taps, grad_bias):
    width = dt_a.shape[1]
    length = width - WIDTH
    half = length // 2

    def main(case):
        taps, bias = (dt_a, db_a) if case == 0 else (dt_b, db_b)
        total = natural(case, taps[...] + far[...], length)
        grad_taps[:, :half] = total[:, :half] + came[:, :half]
        grad_taps[:, half:] = total[:, half:]
        grad_bias[...] = channel_line(bias) + came[0:1, half:]

    pick(role[0], main)


def whole_call(kernel, out_shape, *args):
    spec = lambda a: pl.BlockSpec(a.shape, lambda i, s: (0,) * len(a.shape))
    outs = out_shape if isinstance(out_shape, tuple) else (out_shape,)
    return pl.pallas_call(
        kernel,
        out_shape=out_shape,
        grid_spec=pltpu.PrefetchScalarGridSpec(
            num_scalar_prefetch=1,
            grid=(1,),
            in_specs=[spec(a) for a in args[1:]],
            out_specs=tuple(spec(o) for o in outs) if isinstance(out_shape, tuple) else spec(out_shape),
        ),
    )(*args)


def exchange(values):
    return lax.all_to_all(values, RING, split_axis=0, concat_axis=0)


def local(queries, key_stream, value_stream, filters, bias, grad_out):
    ranks = lax.axis_size(RING)
    role = lax.axis_index("half").astype(jnp.int32)[None]
    groups, length = filters.shape
    per = bias.shape[0]
    group = per // groups
    partner = [(i, (i + ranks) % (2 * ranks)) for i in range(2 * ranks)]
    swap = lambda a: lax.ppermute(a, ("half",) + RING, partner)

    line = jnp.pad(bias, (0, WIDTH - per))[None]
    packed = jnp.concatenate([filters, jnp.broadcast_to(line, (groups, WIDTH))], axis=1)
    other = swap(packed)
    x_a, x_b, y = prepare(role, queries, key_stream, value_stream, grad_out, ranks)
    x_a = exchange(x_a)
    x_b = exchange(x_b)
    y = exchange(y)
    lead_taps, follow_taps, offsets = arrange(role, packed, other, per)
    r_a = swap(x_a)
    r_b = swap(x_b)
    one = lead(0, role, x_a, lead_taps, offsets, group)
    one = lead(1, role, x_b, lead_taps, offsets, group, one)
    one = exchange(one)
    two_a, dt_a, db_a = local_part(0, role, x_a, y, follow_taps, offsets, group)
    two_b, dt_b, db_b = local_part(1, role, x_b, y, follow_taps, offsets, group)
    half = jax.ShapeDtypeStruct((groups, length // 2 + WIDTH), F32)
    sent = whole_call(send_kernel, half, role, dt_a, dt_b, db_a, db_b)
    came = swap(sent)
    two_a = cross_part(0, role, r_a, follow_taps, two_a, group)
    two_a = exchange(two_a)
    two_b = cross_part(1, role, r_b, follow_taps, two_b, group)
    two_b = exchange(two_b)
    far = remote_part(role, x_a, x_b, r_a, r_b, follow_taps, group)
    grad_filters, grad_bias = whole_call(
        receive_kernel,
        (jax.ShapeDtypeStruct((groups, length), F32), jax.ShapeDtypeStruct((1, WIDTH), F32)),
        role, dt_a, dt_b, db_a, db_b, far, came,
    )
    outs = finish(role, queries, key_stream, value_stream, grad_out, one, two_a, two_b, ranks)
    return (*outs, grad_filters, grad_bias[0, :per])


def solution(mesh):
    ctx, dp = mesh.devices.shape
    split = Mesh(mesh.devices.reshape(2, ctx // 2, dp), ("half", "ctx_low", "dp"))
    axes = ("half", "ctx_low", "dp")
    stream = P(None, axes)
    return jax.shard_map(
        local,
        mesh=split,
        in_specs=(stream, stream, stream, P(axes, None), P(axes), stream),
        out_specs=(stream, stream, stream, stream, P(axes, None), P(axes)),
        check_vma=False,
    )
```

```python
import functools

import jax
import jax.numpy as jnp
from jax import lax
from jax.experimental import pallas as pl
from jax.experimental.pallas import tpu as pltpu
from jax.sharding import Mesh, PartitionSpec as P


F32 = jnp.float32
BF16 = jnp.bfloat16
WIDTH = 128
WIDE = 2 * WIDTH
TIMES = (((1,), (0,)), ((), ()))
TIMES_T = (((1,), (1,)), ((), ()))
RING = ("ctx_low", "dp")
TAP_PARTS = 2
STEPS = 2
MANY = 4
SWEEP = 4
UNROLL = 16


def pick(role, cases):
    for case in (0, 1):
        pl.when(role == case)(functools.partial(cases, case))


def prepare_kernel(role, q, k, v, g, first, own):
    def main(case):
        product = (k[...].astype(F32) * v[...].astype(F32)).astype(BF16)
        weighted = (q[...].astype(F32) * g[...].astype(F32)).astype(BF16)
        x, y = (product, weighted) if case == 0 else (weighted, product)
        for part in (0, 1):
            first[:, part] = x[part]
            own[:, part] = y[part]

    pick(role[0], main)


def prepare(role, q, k, v, g, ranks):
    channels, tokens = q.shape
    per = channels // (2 * ranks)
    view = lambda a: a.reshape(2, ranks, per, tokens)
    step = ranks // STEPS
    spec = pl.BlockSpec((2, step, per, tokens), lambda h, r: (0, h, 0, 0))
    out_spec = pl.BlockSpec((step, 2, per, tokens), lambda h, r: (h, 0, 0, 0))
    return pl.pallas_call(
        prepare_kernel,
        out_shape=(jax.ShapeDtypeStruct((ranks, 2, per, tokens), BF16),) * 2,
        grid_spec=pltpu.PrefetchScalarGridSpec(
            num_scalar_prefetch=1,
            grid=(STEPS,),
            in_specs=[spec] * 4,
            out_specs=(out_spec,) * 2,
        ),
        name="prepare",
    )(role, view(q), view(k), view(v), view(g))


def finish_kernel(role, q, k, v, g, one, two, out, gq, gk, gv):
    def main(case):
        for part in (0, 1):
            first, second = one[:, part].astype(F32), two[:, part].astype(F32)
            mixed, back = (first, second) if case == 0 else (second, first)
            out[part] = (q[part].astype(F32) * mixed).astype(BF16)
            gq[part] = (g[part].astype(F32) * mixed).astype(BF16)
            gk[part] = (back * v[part].astype(F32)).astype(BF16)
            gv[part] = (back * k[part].astype(F32)).astype(BF16)

    pick(role[0], main)


def finish(role, q, k, v, g, one, two, ranks):
    channels, tokens = q.shape
    per = channels // (2 * ranks)
    view = lambda a: a.reshape(2, ranks, per, tokens)
    step = ranks // STEPS
    spec = pl.BlockSpec((2, step, per, tokens), lambda h, r: (0, h, 0, 0))
    outs = pl.pallas_call(
        finish_kernel,
        out_shape=(jax.ShapeDtypeStruct((2, ranks, per, tokens), BF16),) * 4,
        grid_spec=pltpu.PrefetchScalarGridSpec(
            num_scalar_prefetch=1,
            grid=(STEPS,),
            in_specs=[spec] * 4
            + [pl.BlockSpec((step, 2, per, tokens), lambda h, r: (h, 0, 0, 0))] * 2,
            out_specs=(spec,) * 4,
        ),
        name="finish",
    )(role, view(q), view(k), view(v), view(g), one, two)
    return [o.reshape(channels, tokens) for o in outs]


def sweep(count, body):
    lax.fori_loop(0, count, lambda n, none: (body(n), none)[1], 0, unroll=min(count, SWEEP))


def build_band(line_of, tiles, case, lags):
    total = tiles[0].shape[1] // WIDTH - 1
    first = 0 if case == 0 else total - lags
    chunk = min(lags, 32)

    def step(c):
        c = c * chunk + first
        if isinstance(c, int):
            line = line_of(slice(c * WIDTH, (c + chunk + 1) * WIDTH))
        else:
            line = line_of(pl.ds(pl.multiple_of(c * WIDTH, WIDTH), (chunk + 1) * WIDTH))
        line = jnp.broadcast_to(line, (WIDTH, (chunk + 1) * WIDTH))
        band = pltpu.roll(line, 0, 1, stride=1, stride_axis=0)[:, WIDTH:]
        place = pl.ds(pl.multiple_of((c + 1) * WIDTH, WIDTH), chunk * WIDTH)
        top = band.astype(BF16)
        tiles[0][:, place] = top
        if len(tiles) > 1:
            tiles[1][:, place] = (band - top.astype(F32)).astype(BF16)

    if lags == chunk:
        step(0)
    else:
        lax.fori_loop(0, lags // chunk, lambda c, none: (step(c), none)[1], 0)


def square_of(tiles, case, d, turned):
    total = tiles.shape[1] // WIDTH - 1

    def tile(lag):
        if isinstance(d, int) and lag < 0:
            return jnp.zeros((WIDTH, WIDTH), BF16)
        at = lag + 1 if case == 0 else total - lag
        if isinstance(d, int):
            return tiles[:, at * WIDTH : (at + 1) * WIDTH]
        value = tiles[:, pl.ds(pl.multiple_of(jnp.clip(at, 0, total) * WIDTH, WIDTH), WIDTH)]
        return jnp.where(lag < 0, jnp.zeros_like(value), value)

    mid, less, more = tile(2 * d), tile(2 * d - 1), tile(2 * d + 1)
    if turned:
        less, more = more, less
    return jnp.concatenate(
        [jnp.concatenate([mid, more], axis=1), jnp.concatenate([less, mid], axis=1)], axis=0
    )


def dot(a, b, form=TIMES):
    return lax.dot_general(a, b, form, preferred_element_type=F32)


def gather_rows(case, src, dst, start, blocks, group):
    for i in range(blocks):
        at = i if case == 0 else blocks - 1 - i
        row = start + (i // 2) * group
        col = (i % 2) * WIDTH
        dst[row : row + group, col : col + WIDTH] = src[at]


def scatter_rows(case, value, dst, blocks, group):
    for i in range(blocks):
        at = i if case == 0 else blocks - 1 - i
        row = (i // 2) * group
        col = (i % 2) * WIDTH
        dst[at] = value[row : row + group, col : col + WIDTH].astype(BF16)


def apply_band(data, start, sign, shift, lags, tiles, case, turned, acc, group, base=None):
    rows = acc.shape[0]
    pairs = rows // group
    if pairs <= UNROLL:
        sums = [None] * pairs
        if base is not None:
            sums = [base[i * group : (i + 1) * group, :] for i in range(pairs)]
        for d in range(*lags):
            at = [i for i in range(pairs) if 0 <= i + sign * d + shift < pairs]
            low = start + (at[0] + sign * d + shift) * group
            block = data[low : low + len(at) * group, :]
            for part in tiles:
                found = dot(block, square_of(part, case, d, turned))
                for k, i in enumerate(at):
                    piece = found[k * group : (k + 1) * group]
                    sums[i] = piece if sums[i] is None else sums[i] + piece
        return jnp.concatenate(sums, axis=0)
    acc[...] = jnp.zeros_like(acc) if base is None else base[...]

    def step(d, none):
        low = pl.multiple_of(start + (sign * d + shift) * group, group)
        block = data[pl.ds(low, rows), :]
        for part in tiles:
            acc[...] += dot(block, square_of(part, case, d, turned))
        return none

    lax.fori_loop(*lags, step, 0)
    return acc[...]


def bias_term(data, bias, pairs, group):
    line = jnp.concatenate([bias, bias], axis=1)
    shaped = data.astype(F32).reshape(pairs, group, WIDE) * line[None]
    return shaped.reshape(pairs * group, WIDE)


def gather_line(case, src, dst, start, blocks, group):
    for i in range(blocks):
        at = i if case == 0 else blocks - 1 - i
        dst[start + i * group : start + (i + 1) * group, :] = src[at]


def flip_rows(data):
    down = lax.broadcasted_iota(jnp.int32, (WIDTH, WIDTH), 0)
    across = lax.broadcasted_iota(jnp.int32, (WIDTH, WIDTH), 1)
    mirror = jnp.where(down + across == WIDTH - 1, 1.0, 0.0).astype(BF16)
    return dot(mirror, data, TIMES_T).astype(BF16)


def correlate(case, turned, data, start, shift, lags, total, lines, group):
    rows = turned.shape[1]
    inside = lax.broadcasted_iota(jnp.int32, (WIDTH, WIDTH), 1) <= lax.broadcasted_iota(
        jnp.int32, (WIDTH, WIDTH), 0
    )

    def step(lag):
        low = start + (lag + shift) * group
        if not isinstance(lag, int):
            low = pl.multiple_of(low, group)
        square = dot(turned, data[pl.ds(low, rows), :])
        flat = pltpu.roll(square, 1, 1, stride=1, stride_axis=0)
        kept = jnp.where(inside, flat, 0.0)
        at = lag + 1 if case == 0 else total - lag
        kept = jnp.sum(kept.reshape(WIDTH // 8, 8, WIDTH), axis=0)
        lines[at] += kept
        lines[at - 1] += jnp.sum(flat.reshape(WIDTH // 8, 8, WIDTH), axis=0) - kept

    if rows // group <= 2 * UNROLL:
        for lag in range(*lags):
            step(lag)
    else:
        lax.fori_loop(*lags, lambda lag, none: (step(lag), none)[1], 0)


def fold_lines(lines, dtaps, row):
    here = lax.broadcasted_iota(jnp.int32, (dtaps.shape[0], WIDTH), 0) == row
    for j in range(lines.shape[0]):
        lanes = slice(j * WIDTH, (j + 1) * WIDTH)
        total = jnp.broadcast_to(jnp.sum(lines[j], axis=0, keepdims=True), here.shape)
        dtaps[:, lanes] = jnp.where(here, total, dtaps[:, lanes])


def row_at(many, n):
    return pl.program_id(1) * many + n


def row_of(taps, many, n):
    row = row_at(many, n)
    return lambda lanes: taps[pl.ds(row, 1), lanes]


def lead_kernel(blocks, group, many, role, x, taps, bias, out, xs, acc, *tiles):
    pairs = blocks // 2
    rows = pairs * group

    def each(case, n):
        place = pl.ds(pl.multiple_of(n * group, group), group)
        line, band = xs, tiles
        line[0:rows, :] = jnp.zeros((rows, WIDE), BF16)
        gather_rows(case, x.at[:, place], line, rows, blocks, group)
        build_band(row_of(taps, many, n), band, case, blocks)
        value = apply_band(line, rows, -1, 0, (0, pairs), band, case, False, acc, group)
        value += bias_term(line[rows : 2 * rows, :], bias[place], pairs, group)
        scatter_rows(case, value, out.at[:, place], blocks, group)

    pick(role[0], lambda case: sweep(many, functools.partial(each, case)))


def local_kernel(
    blocks, group, many, role, x, y, taps, bias, out, dtaps, dbias, xs, ys, yl, acc, lines, *tiles
):
    pairs = blocks // 2
    rows = pairs * group

    def each(case, n):
        place = pl.ds(pl.multiple_of(n * group, group), group)
        ys[rows : 2 * rows, :] = jnp.zeros((rows, WIDE), BF16)
        yl[2 * rows : 4 * rows, :] = jnp.zeros((2 * rows, WIDTH), BF16)
        gather_line(case, x.at[:, place], xs, 0, blocks, group)
        gather_rows(case, y.at[:, place], ys, 0, blocks, group)
        gather_line(case, y.at[:, place], yl, 0, blocks, group)
        build_band(row_of(taps, many, n), tiles, 1 - case, blocks)
        value = apply_band(ys, 0, 1, 0, (0, pairs), tiles, 1 - case, True, acc, group)
        out[n] = value + bias_term(ys[0:rows, :], bias[place], pairs, group)
        both = xs[...].astype(F32) * yl[0 : 2 * rows, :].astype(F32)
        dbias[place] = jnp.sum(both.reshape(blocks, group, WIDTH), axis=0)
        lines[...] = jnp.zeros_like(lines)
        correlate(case, flip_rows(xs[...]), yl, 0, 0, (0, blocks), 2 * blocks, lines, group)
        fold_lines(lines, dtaps, row_at(many, n))

    pick(role[0], lambda case: sweep(many, functools.partial(each, case)))


def cross_kernel(blocks, group, many, role, r_a, r_b, taps, base, out, rs, acc, *tiles):
    pairs = blocks // 2
    rows = pairs * group

    def each(case, n):
        place = pl.ds(pl.multiple_of(n * group, group), group)
        zeros = jnp.zeros((rows, WIDE), BF16)
        rs[0:rows, :] = zeros
        rs[2 * rows : 3 * rows, :] = zeros
        begins = pl.program_id(0) == 0
        for i in range(blocks):
            at = i if case == 0 else blocks - 1 - i
            row = rows + (i // 2) * group
            col = (i % 2) * WIDTH
            tile = jnp.where(begins, r_a[at, place, :], r_b[at, place, :])
            rs[row : row + group, col : col + WIDTH] = tile
        build_band(row_of(taps, many, n), tiles, 1 - case, 2 * blocks)
        value = apply_band(
            rs, rows, 1, -pairs, (1, 2 * pairs), tiles, 1 - case, True, acc, group, base.at[n]
        )
        scatter_rows(case, value, out.at[:, place], blocks, group)

    pick(role[0], lambda case: sweep(many, functools.partial(each, case)))


def remote_kernel(blocks, group, many, role, x, r_a, r_b, dtaps, xs, rl, lines):
    rows = blocks * group

    def each(case, n):
        place = pl.ds(pl.multiple_of(n * group, group), group)
        zeros = jnp.zeros((rows, WIDTH), BF16)
        rl[0:rows, :] = zeros
        rl[2 * rows : 3 * rows, :] = zeros
        gather_line(case, x.at[:, case, place], xs, 0, blocks, group)
        r = r_a if case == 0 else r_b
        gather_line(case, r.at[:, place], rl, rows, blocks, group)
        lines[...] = jnp.zeros_like(lines)
        correlate(
            case, flip_rows(xs[...]), rl, rows, -blocks, (1, 2 * blocks), 2 * blocks, lines, group
        )
        fold_lines(lines, dtaps, row_at(many, n))

    pick(role[0], lambda case: sweep(many, functools.partial(each, case)))


class Sizes:
    def __init__(self, x, taps, group):
        self.group = group
        self.blocks, _, self.per, self.tokens = x.shape
        self.groups, self.width = taps.shape[1:]
        self.many = min(self.groups, MANY)
        self.rows = self.blocks // 2 * group
        self.data = pl.BlockSpec(
            (self.blocks, None, self.many * group, self.tokens), lambda p, i, s: (0, p, i, 0)
        )
        self.both = pl.BlockSpec(
            (self.blocks, 2, self.many * group, self.tokens), lambda p, i, s: (0, 0, i, 0)
        )
        self.bands = [pltpu.VMEM((WIDTH, self.width), BF16)] * TAP_PARTS
        self.acc = pltpu.VMEM((self.rows, WIDE), F32)
        self.lines = pltpu.VMEM((self.width // WIDTH, 8, WIDTH), F32)
        self.stream = jax.ShapeDtypeStruct(x.shape, BF16)
        self.sums = jax.ShapeDtypeStruct((2, self.groups, self.rows, WIDE), F32)
        self.sums_spec = pl.BlockSpec(
            (None, self.many, self.rows, WIDE), lambda p, i, s: (p, i, 0, 0)
        )
        self.taps = pl.BlockSpec((None, self.groups, self.width), lambda p, i, s: (p, 0, 0))
        self.bias = pl.BlockSpec((None, self.many * group, WIDTH), lambda p, i, s: (p, i, 0))

    def held(self, count, width=WIDE):
        return pltpu.VMEM((count * self.rows, width), BF16)

    def dtaps(self, parts):
        return jax.ShapeDtypeStruct((parts, self.groups, self.width), F32)

    def call(self, kernel, parts, out_shape, in_specs, out_specs, scratch, share):
        work = 4 * self.groups * self.group * (self.blocks * self.tokens) ** 2
        return pl.pallas_call(
            functools.partial(kernel, self.blocks, self.group, self.many),
            out_shape=out_shape,
            grid_spec=pltpu.PrefetchScalarGridSpec(
                num_scalar_prefetch=1,
                grid=(parts, self.groups // self.many),
                in_specs=in_specs,
                out_specs=out_specs,
                scratch_shapes=scratch,
            ),
            cost_estimate=pl.CostEstimate(
                flops=int(share * work),
                bytes_accessed=8 * self.blocks * self.per * self.tokens,
                transcendentals=0,
            ),
        )


def lead(role, x, taps, bias, group):
    z = Sizes(x, taps, group)
    return z.call(
        lead_kernel, 2, z.stream, [z.data, z.taps, z.bias], z.data,
        [z.held(2), z.acc] + z.bands, 1,
    )(role, x, taps, bias)


def local_part(role, x, y, taps, bias, group):
    z = Sizes(x, taps, group)
    return z.call(
        local_kernel, 2,
        (z.sums, z.dtaps(2), jax.ShapeDtypeStruct((2, z.per, WIDTH), F32)),
        [z.data, z.data, z.taps, z.bias],
        (z.sums_spec, z.taps, z.bias),
        [z.held(2, WIDTH), z.held(2), z.held(4, WIDTH), z.acc, z.lines] + z.bands, 1.5,
    )(role, x, y, taps, bias)


def cross_part(role, x, r_a, r_b, taps, base, group):
    z = Sizes(x, taps, group)
    last = z.groups // z.many - 1
    shape = (z.blocks, z.many * group, z.tokens)
    spec_a = pl.BlockSpec(shape, lambda p, i, s: (0, jnp.where(p == 0, i, last), 0))
    spec_b = pl.BlockSpec(shape, lambda p, i, s: (0, jnp.where(p == 1, i, 0), 0))
    return z.call(
        cross_kernel, 2, z.stream, [spec_a, spec_b, z.taps, z.sums_spec], z.data,
        [z.held(3), z.acc] + z.bands, 2,
    )(role, r_a, r_b, taps, base)


def remote_part(role, x, r_a, r_b, taps, group):
    z = Sizes(x, taps, group)
    spec = pl.BlockSpec((z.blocks, z.many * group, z.tokens), lambda p, i, s: (0, i, 0))
    return z.call(
        remote_kernel, 1, z.dtaps(1), [z.both, spec, spec], z.taps,
        [z.held(2, WIDTH), z.held(6, WIDTH), z.lines], 1,
    )(role, x, r_a, r_b)


def exact_parts(data):
    high = data.astype(BF16)
    rest = data - high.astype(F32)
    middle = rest.astype(BF16)
    return high, middle, (rest - middle.astype(F32)).astype(BF16)


def reverse_line(data, length, count):
    rows, width = data.shape
    total = length // WIDTH
    down = lax.broadcasted_iota(jnp.int32, (WIDTH, WIDTH), 0)
    across = lax.broadcasted_iota(jnp.int32, (WIDTH, WIDTH), 1)
    inner = jnp.where(down + across == WIDTH, 1.0, 0.0).astype(BF16)
    edge = jnp.where(down + across == 0, 1.0, 0.0).astype(BF16)
    zero = jnp.zeros((rows, WIDTH), F32)

    def block(t):
        return data[:, t * WIDTH : (t + 1) * WIDTH] if 0 <= t < width // WIDTH else zero

    done = []
    for j in range(count // WIDTH):
        found = zero
        for a, b in zip(exact_parts(block(total - 1 - j)), exact_parts(block(total - j))):
            found += dot(a, inner) + dot(b, edge)
        done.append(found)
    return jnp.concatenate(done, axis=1)


def arrange_kernel(role, mine, other, my_bias, other_bias, lead_taps, follow_taps, bias):
    groups, length = mine.shape

    def main(case):
        for part in (0, 1):
            taps = (mine if part == case else other)[...]
            ahead = jnp.concatenate([jnp.zeros((groups, WIDTH), F32), taps], axis=1)
            behind = reverse_line(taps, length, length + WIDTH)
            first, second = (ahead, behind) if case == 0 else (behind, ahead)
            lead_taps[part] = first
            follow_taps[part] = second
            line = (my_bias if part == case else other_bias)[...]
            bias[part] = jnp.broadcast_to(line, (WIDTH, line.shape[1])).T

    pick(role[0], main)


def natural(case, dtaps, count):
    if case == 0:
        return dtaps[:, WIDTH : WIDTH + count]
    return reverse_line(dtaps, dtaps.shape[1] - WIDTH, count)


def channel_line(dbias):
    square = dbias[...]
    if square.shape[0] < WIDTH:
        square = jnp.concatenate(
            [square, jnp.zeros((WIDTH - square.shape[0], WIDTH), F32)], axis=0
        )
    return jnp.sum(square.T, axis=0, keepdims=True)


def send_kernel(role, dtaps, dbias, sent):
    _, groups, width = dtaps.shape
    half = (width - WIDTH) // 2

    def main(case):
        sent[:, :half] = natural(case, dtaps[1 - case], half)
        sent[:, half:] = jnp.broadcast_to(channel_line(dbias.at[1 - case]), (groups, WIDTH))

    pick(role[0], main)


def receive_kernel(role, dtaps, dbias, far, came, grad_taps, grad_bias):
    length = dtaps.shape[2] - WIDTH
    half = length // 2

    def main(case):
        total = natural(case, dtaps[case] + far[0], length)
        grad_taps[:, :half] = total[:, :half] + came[:, :half]
        grad_taps[:, half:] = total[:, half:]
        grad_bias[...] = channel_line(dbias.at[case]) + came[0:1, half:]

    pick(role[0], main)


def whole_call(kernel, out_shape, *args):
    spec = lambda a: pl.BlockSpec(a.shape, lambda i, s: (0,) * len(a.shape))
    outs = out_shape if isinstance(out_shape, tuple) else (out_shape,)
    return pl.pallas_call(
        kernel,
        out_shape=out_shape,
        grid_spec=pltpu.PrefetchScalarGridSpec(
            num_scalar_prefetch=1,
            grid=(1,),
            in_specs=[spec(a) for a in args[1:]],
            out_specs=tuple(spec(o) for o in outs) if isinstance(out_shape, tuple) else spec(out_shape),
        ),
    )(*args)


def exchange(values):
    return lax.all_to_all(values, RING, split_axis=0, concat_axis=0)


def local(queries, key_stream, value_stream, filters, bias, grad_out):
    ranks = lax.axis_size(RING)
    role = lax.axis_index("half").astype(jnp.int32)[None]
    groups, length = filters.shape
    per = bias.shape[0]
    group = per // groups
    partner = [(i, (i + ranks) % (2 * ranks)) for i in range(2 * ranks)]
    swap = lambda a: lax.ppermute(a, ("half",) + RING, partner)

    bias = bias[None]
    other = swap(filters)
    other_bias = swap(bias)
    x, y = prepare(role, queries, key_stream, value_stream, grad_out, ranks)
    x = exchange(x)
    y = exchange(y)
    taps = jax.ShapeDtypeStruct((2, groups, length + WIDTH), F32)
    lead_taps, follow_taps, offsets = whole_call(
        arrange_kernel,
        (taps, taps, jax.ShapeDtypeStruct((2, per, WIDTH), F32)),
        role, filters, other, bias, other_bias,
    )
    r_a = swap(x[:, 0])
    r_b = swap(x[:, 1])
    one = lead(role, x, lead_taps, offsets, group)
    one = exchange(one)
    two, dtaps, dbias = local_part(role, x, y, follow_taps, offsets, group)
    half = jax.ShapeDtypeStruct((groups, length // 2 + WIDTH), F32)
    sent = whole_call(send_kernel, half, role, dtaps, dbias)
    came = swap(sent)
    two = cross_part(role, x, r_a, r_b, follow_taps, two, group)
    two = exchange(two)
    far = remote_part(role, x, r_a, r_b, follow_taps, group)
    grad_filters, grad_bias = whole_call(
        receive_kernel,
        (jax.ShapeDtypeStruct((groups, length), F32), jax.ShapeDtypeStruct((1, WIDTH), F32)),
        role, dtaps, dbias, far, came,
    )
    outs = finish(role, queries, key_stream, value_stream, grad_out, one, two, ranks)
    return (*outs, grad_filters, grad_bias[0, :per])


def solution(mesh):
    ctx, dp = mesh.devices.shape
    split = Mesh(mesh.devices.reshape(2, ctx // 2, dp), ("half", "ctx_low", "dp"))
    axes = ("half", "ctx_low", "dp")
    stream = P(None, axes)
    return jax.shard_map(
        local,
        mesh=split,
        in_specs=(stream, stream, stream, P(axes, None), P(axes), stream),
        out_specs=(stream, stream, stream, stream, P(axes, None), P(axes)),
        check_vma=False,
    )
```

```python
import functools

import jax
import jax.numpy as jnp
from jax import lax
from jax.experimental import pallas as pl
from jax.experimental.pallas import tpu as pltpu
from jax.sharding import Mesh, PartitionSpec as P


F32 = jnp.float32
BF16 = jnp.bfloat16
WIDTH = 128
WIDE = 2 * WIDTH
TIMES = (((1,), (0,)), ((), ()))
TIMES_T = (((1,), (1,)), ((), ()))
RING = ("ctx_low", "dp")
TAP_PARTS = 2
STEPS = 2
MANY = 4
SWEEP = 4
UNROLL = 16


def pick(role, cases):
    for case in (0, 1):
        pl.when(role == case)(functools.partial(cases, case))


def prepare_kernel(other, role, q, k, v, g, out):
    def main(case):
        one, two = (k, v) if case == other else (q, g)
        made = (one[...].astype(F32) * two[...].astype(F32)).astype(BF16)
        for part in (0, 1):
            out[:, part] = made[part]

    pick(role[0], main)


def prepare(other, role, q, k, v, g, ranks):
    channels, tokens = q.shape
    per = channels // (2 * ranks)
    view = lambda a: a.reshape(2, ranks, per, tokens)
    step = ranks // STEPS
    block = (2, step, per, tokens)
    used = pl.BlockSpec(block, lambda h, r: (0, jnp.where(r[0] == other, h, 0), 0, 0))
    rest = pl.BlockSpec(block, lambda h, r: (0, jnp.where(r[0] == other, 0, h), 0, 0))
    return pl.pallas_call(
        functools.partial(prepare_kernel, other),
        out_shape=jax.ShapeDtypeStruct((ranks, 2, per, tokens), BF16),
        grid_spec=pltpu.PrefetchScalarGridSpec(
            num_scalar_prefetch=1,
            grid=(STEPS,),
            in_specs=[rest, used, used, rest],
            out_specs=pl.BlockSpec((step, 2, per, tokens), lambda h, r: (h, 0, 0, 0)),
        ),
        name="prepare",
    )(role, view(q), view(k), view(v), view(g))


def finish_kernel(role, q, k, v, g, one, two, out, gq, gk, gv):
    def main(case):
        for part in (0, 1):
            first, second = one[:, part].astype(F32), two[:, part].astype(F32)
            mixed, back = (first, second) if case == 0 else (second, first)
            out[part] = (q[part].astype(F32) * mixed).astype(BF16)
            gq[part] = (g[part].astype(F32) * mixed).astype(BF16)
            gk[part] = (back * v[part].astype(F32)).astype(BF16)
            gv[part] = (back * k[part].astype(F32)).astype(BF16)

    pick(role[0], main)


def finish(role, q, k, v, g, one, two, ranks):
    channels, tokens = q.shape
    per = channels // (2 * ranks)
    view = lambda a: a.reshape(2, ranks, per, tokens)
    step = ranks // STEPS
    spec = pl.BlockSpec((2, step, per, tokens), lambda h, r: (0, h, 0, 0))
    outs = pl.pallas_call(
        finish_kernel,
        out_shape=(jax.ShapeDtypeStruct((2, ranks, per, tokens), BF16),) * 4,
        grid_spec=pltpu.PrefetchScalarGridSpec(
            num_scalar_prefetch=1,
            grid=(STEPS,),
            in_specs=[spec] * 4
            + [pl.BlockSpec((step, 2, per, tokens), lambda h, r: (h, 0, 0, 0))] * 2,
            out_specs=(spec,) * 4,
        ),
        name="finish",
    )(role, view(q), view(k), view(v), view(g), one, two)
    return [o.reshape(channels, tokens) for o in outs]


def sweep(count, body):
    lax.fori_loop(0, count, lambda n, none: (body(n), none)[1], 0, unroll=min(count, SWEEP))


def build_band(line_of, tiles, case, lags):
    total = tiles[0].shape[1] // WIDTH - 1
    first = 0 if case == 0 else total - lags
    chunk = min(lags, 32)

    def step(c):
        c = c * chunk + first
        if isinstance(c, int):
            line = line_of(slice(c * WIDTH, (c + chunk + 1) * WIDTH))
        else:
            line = line_of(pl.ds(pl.multiple_of(c * WIDTH, WIDTH), (chunk + 1) * WIDTH))
        line = jnp.broadcast_to(line, (WIDTH, (chunk + 1) * WIDTH))
        band = pltpu.roll(line, 0, 1, stride=1, stride_axis=0)[:, WIDTH:]
        place = pl.ds(pl.multiple_of((c + 1) * WIDTH, WIDTH), chunk * WIDTH)
        top = band.astype(BF16)
        tiles[0][:, place] = top
        if len(tiles) > 1:
            tiles[1][:, place] = (band - top.astype(F32)).astype(BF16)

    if lags == chunk:
        step(0)
    else:
        lax.fori_loop(0, lags // chunk, lambda c, none: (step(c), none)[1], 0)


def square_of(tiles, case, d, turned):
    total = tiles.shape[1] // WIDTH - 1

    def tile(lag):
        if isinstance(d, int) and lag < 0:
            return jnp.zeros((WIDTH, WIDTH), BF16)
        at = lag + 1 if case == 0 else total - lag
        if isinstance(d, int):
            return tiles[:, at * WIDTH : (at + 1) * WIDTH]
        value = tiles[:, pl.ds(pl.multiple_of(jnp.clip(at, 0, total) * WIDTH, WIDTH), WIDTH)]
        return jnp.where(lag < 0, jnp.zeros_like(value), value)

    mid, less, more = tile(2 * d), tile(2 * d - 1), tile(2 * d + 1)
    if turned:
        less, more = more, less
    return jnp.concatenate(
        [jnp.concatenate([mid, more], axis=1), jnp.concatenate([less, mid], axis=1)], axis=0
    )


def dot(a, b, form=TIMES):
    return lax.dot_general(a, b, form, preferred_element_type=F32)


def gather_rows(case, src, dst, start, blocks, group):
    for i in range(blocks):
        at = i if case == 0 else blocks - 1 - i
        row = start + (i // 2) * group
        col = (i % 2) * WIDTH
        dst[row : row + group, col : col + WIDTH] = src[at]


def scatter_rows(case, value, dst, blocks, group):
    for i in range(blocks):
        at = i if case == 0 else blocks - 1 - i
        row = (i // 2) * group
        col = (i % 2) * WIDTH
        dst[at] = value[row : row + group, col : col + WIDTH].astype(BF16)


def apply_band(data, start, sign, shift, lags, tiles, case, turned, acc, group, base=None):
    rows = acc.shape[0]
    pairs = rows // group
    if pairs <= UNROLL:
        sums = [None] * pairs
        if base is not None:
            sums = [base[i * group : (i + 1) * group, :] for i in range(pairs)]
        for d in range(*lags):
            at = [i for i in range(pairs) if 0 <= i + sign * d + shift < pairs]
            low = start + (at[0] + sign * d + shift) * group
            block = data[low : low + len(at) * group, :]
            for part in tiles:
                found = dot(block, square_of(part, case, d, turned))
                for k, i in enumerate(at):
                    piece = found[k * group : (k + 1) * group]
                    sums[i] = piece if sums[i] is None else sums[i] + piece
        return jnp.concatenate(sums, axis=0)
    acc[...] = jnp.zeros_like(acc) if base is None else base[...]

    def step(d, none):
        low = pl.multiple_of(start + (sign * d + shift) * group, group)
        block = data[pl.ds(low, rows), :]
        for part in tiles:
            acc[...] += dot(block, square_of(part, case, d, turned))
        return none

    lax.fori_loop(*lags, step, 0)
    return acc[...]


def bias_term(data, bias, pairs, group):
    line = jnp.concatenate([bias, bias], axis=1)
    shaped = data.astype(F32).reshape(pairs, group, WIDE) * line[None]
    return shaped.reshape(pairs * group, WIDE)


def gather_line(case, src, dst, start, blocks, group):
    for i in range(blocks):
        at = i if case == 0 else blocks - 1 - i
        dst[start + i * group : start + (i + 1) * group, :] = src[at]


def flip_rows(data):
    down = lax.broadcasted_iota(jnp.int32, (WIDTH, WIDTH), 0)
    across = lax.broadcasted_iota(jnp.int32, (WIDTH, WIDTH), 1)
    mirror = jnp.where(down + across == WIDTH - 1, 1.0, 0.0).astype(BF16)
    return dot(mirror, data, TIMES_T).astype(BF16)


def correlate(case, turned, data, start, shift, lags, total, lines, group):
    rows = turned.shape[1]
    inside = lax.broadcasted_iota(jnp.int32, (WIDTH, WIDTH), 1) <= lax.broadcasted_iota(
        jnp.int32, (WIDTH, WIDTH), 0
    )

    def step(lag):
        low = start + (lag + shift) * group
        if not isinstance(lag, int):
            low = pl.multiple_of(low, group)
        square = dot(turned, data[pl.ds(low, rows), :])
        flat = pltpu.roll(square, 1, 1, stride=1, stride_axis=0)
        kept = jnp.where(inside, flat, 0.0)
        at = lag + 1 if case == 0 else total - lag
        kept = jnp.sum(kept.reshape(WIDTH // 8, 8, WIDTH), axis=0)
        lines[at] += kept
        lines[at - 1] += jnp.sum(flat.reshape(WIDTH // 8, 8, WIDTH), axis=0) - kept

    if rows // group <= 2 * UNROLL:
        for lag in range(*lags):
            step(lag)
    else:
        lax.fori_loop(*lags, lambda lag, none: (step(lag), none)[1], 0)


def fold_lines(lines, dtaps, row):
    here = lax.broadcasted_iota(jnp.int32, (dtaps.shape[0], WIDTH), 0) == row
    for j in range(lines.shape[0]):
        lanes = slice(j * WIDTH, (j + 1) * WIDTH)
        total = jnp.broadcast_to(jnp.sum(lines[j], axis=0, keepdims=True), here.shape)
        dtaps[:, lanes] = jnp.where(here, total, dtaps[:, lanes])


def row_at(many, n):
    return pl.program_id(1) * many + n


def row_of(taps, many, n):
    row = row_at(many, n)
    return lambda lanes: taps[pl.ds(row, 1), lanes]


def lead_kernel(blocks, group, many, role, x, taps, bias, out, xs, acc, *tiles):
    pairs = blocks // 2
    rows = pairs * group

    def each(case, n):
        place = pl.ds(pl.multiple_of(n * group, group), group)
        line, band = xs, tiles
        line[0:rows, :] = jnp.zeros((rows, WIDE), BF16)
        gather_rows(case, x.at[:, place], line, rows, blocks, group)
        build_band(row_of(taps, many, n), band, case, blocks)
        value = apply_band(line, rows, -1, 0, (0, pairs), band, case, False, acc, group)
        value += bias_term(line[rows : 2 * rows, :], bias[place], pairs, group)
        scatter_rows(case, value, out.at[:, place], blocks, group)

    pick(role[0], lambda case: sweep(many, functools.partial(each, case)))


def local_kernel(
    blocks, group, many, role, x, y, taps, bias, out, dtaps, dbias, xs, ys, yl, acc, lines, *tiles
):
    pairs = blocks // 2
    rows = pairs * group

    def each(case, n):
        place = pl.ds(pl.multiple_of(n * group, group), group)
        ys[rows : 2 * rows, :] = jnp.zeros((rows, WIDE), BF16)
        yl[2 * rows : 4 * rows, :] = jnp.zeros((2 * rows, WIDTH), BF16)
        gather_line(case, x.at[:, place], xs, 0, blocks, group)
        gather_rows(case, y.at[:, place], ys, 0, blocks, group)
        gather_line(case, y.at[:, place], yl, 0, blocks, group)
        build_band(row_of(taps, many, n), tiles, 1 - case, blocks)
        value = apply_band(ys, 0, 1, 0, (0, pairs), tiles, 1 - case, True, acc, group)
        out[n] = value + bias_term(ys[0:rows, :], bias[place], pairs, group)
        both = xs[...].astype(F32) * yl[0 : 2 * rows, :].astype(F32)
        dbias[place] = jnp.sum(both.reshape(blocks, group, WIDTH), axis=0)
        lines[...] = jnp.zeros_like(lines)
        correlate(case, flip_rows(xs[...]), yl, 0, 0, (0, blocks), 2 * blocks, lines, group)
        fold_lines(lines, dtaps, row_at(many, n))

    pick(role[0], lambda case: sweep(many, functools.partial(each, case)))


def cross_kernel(blocks, group, many, role, r_a, r_b, taps, base, out, rs, acc, *tiles):
    pairs = blocks // 2
    rows = pairs * group

    def each(case, n):
        place = pl.ds(pl.multiple_of(n * group, group), group)
        zeros = jnp.zeros((rows, WIDE), BF16)
        rs[0:rows, :] = zeros
        rs[2 * rows : 3 * rows, :] = zeros
        begins = pl.program_id(0) == 0
        for i in range(blocks):
            at = i if case == 0 else blocks - 1 - i
            row = rows + (i // 2) * group
            col = (i % 2) * WIDTH
            tile = jnp.where(begins, r_a[at, place, :], r_b[at, place, :])
            rs[row : row + group, col : col + WIDTH] = tile
        build_band(row_of(taps, many, n), tiles, 1 - case, 2 * blocks)
        value = apply_band(
            rs, rows, 1, -pairs, (1, 2 * pairs), tiles, 1 - case, True, acc, group, base.at[n]
        )
        scatter_rows(case, value, out.at[:, place], blocks, group)

    pick(role[0], lambda case: sweep(many, functools.partial(each, case)))


def remote_kernel(blocks, group, many, role, x, r_a, r_b, dtaps, xs, rl, lines):
    rows = blocks * group

    def each(case, n):
        place = pl.ds(pl.multiple_of(n * group, group), group)
        zeros = jnp.zeros((rows, WIDTH), BF16)
        rl[0:rows, :] = zeros
        rl[2 * rows : 3 * rows, :] = zeros
        gather_line(case, x.at[:, case, place], xs, 0, blocks, group)
        r = r_a if case == 0 else r_b
        gather_line(case, r.at[:, place], rl, rows, blocks, group)
        lines[...] = jnp.zeros_like(lines)
        correlate(
            case, flip_rows(xs[...]), rl, rows, -blocks, (1, 2 * blocks), 2 * blocks, lines, group
        )
        fold_lines(lines, dtaps, row_at(many, n))

    pick(role[0], lambda case: sweep(many, functools.partial(each, case)))


class Sizes:
    def __init__(self, x, taps, group):
        self.group = group
        self.blocks, _, self.per, self.tokens = x.shape
        self.groups, self.width = taps.shape[1:]
        self.many = min(self.groups, MANY)
        self.rows = self.blocks // 2 * group
        self.data = pl.BlockSpec(
            (self.blocks, None, self.many * group, self.tokens), lambda p, i, s: (0, p, i, 0)
        )
        self.both = pl.BlockSpec(
            (self.blocks, 2, self.many * group, self.tokens), lambda p, i, s: (0, 0, i, 0)
        )
        self.bands = [pltpu.VMEM((WIDTH, self.width), BF16)] * TAP_PARTS
        self.acc = pltpu.VMEM((self.rows, WIDE), F32)
        self.lines = pltpu.VMEM((self.width // WIDTH, 8, WIDTH), F32)
        self.stream = jax.ShapeDtypeStruct(x.shape, BF16)
        self.sums = jax.ShapeDtypeStruct((2, self.groups, self.rows, WIDE), F32)
        self.sums_spec = pl.BlockSpec(
            (None, self.many, self.rows, WIDE), lambda p, i, s: (p, i, 0, 0)
        )
        self.taps = pl.BlockSpec((None, self.groups, self.width), lambda p, i, s: (p, 0, 0))
        self.bias = pl.BlockSpec((None, self.many * group, WIDTH), lambda p, i, s: (p, i, 0))

    def held(self, count, width=WIDE):
        return pltpu.VMEM((count * self.rows, width), BF16)

    def dtaps(self, parts):
        return jax.ShapeDtypeStruct((parts, self.groups, self.width), F32)

    def call(self, kernel, parts, out_shape, in_specs, out_specs, scratch, share):
        work = 4 * self.groups * self.group * (self.blocks * self.tokens) ** 2
        return pl.pallas_call(
            functools.partial(kernel, self.blocks, self.group, self.many),
            out_shape=out_shape,
            grid_spec=pltpu.PrefetchScalarGridSpec(
                num_scalar_prefetch=1,
                grid=(parts, self.groups // self.many),
                in_specs=in_specs,
                out_specs=out_specs,
                scratch_shapes=scratch,
            ),
            cost_estimate=pl.CostEstimate(
                flops=int(share * work),
                bytes_accessed=8 * self.blocks * self.per * self.tokens,
                transcendentals=0,
            ),
        )


def lead(role, x, taps, bias, group):
    z = Sizes(x, taps, group)
    return z.call(
        lead_kernel, 2, z.stream, [z.data, z.taps, z.bias], z.data,
        [z.held(2), z.acc] + z.bands, 1,
    )(role, x, taps, bias)


def local_part(role, x, y, taps, bias, group):
    z = Sizes(x, taps, group)
    return z.call(
        local_kernel, 2,
        (z.sums, z.dtaps(2), jax.ShapeDtypeStruct((2, z.per, WIDTH), F32)),
        [z.data, z.data, z.taps, z.bias],
        (z.sums_spec, z.taps, z.bias),
        [z.held(2, WIDTH), z.held(2), z.held(4, WIDTH), z.acc, z.lines] + z.bands, 1.5,
    )(role, x, y, taps, bias)


def cross_part(role, x, r_a, r_b, taps, base, group):
    z = Sizes(x, taps, group)
    last = z.groups // z.many - 1
    shape = (z.blocks, z.many * group, z.tokens)
    spec_a = pl.BlockSpec(shape, lambda p, i, s: (0, jnp.where(p == 0, i, last), 0))
    spec_b = pl.BlockSpec(shape, lambda p, i, s: (0, jnp.where(p == 1, i, 0), 0))
    return z.call(
        cross_kernel, 2, z.stream, [spec_a, spec_b, z.taps, z.sums_spec], z.data,
        [z.held(3), z.acc] + z.bands, 2,
    )(role, r_a, r_b, taps, base)


def remote_part(role, x, r_a, r_b, taps, group):
    z = Sizes(x, taps, group)
    spec = pl.BlockSpec((z.blocks, z.many * group, z.tokens), lambda p, i, s: (0, i, 0))
    return z.call(
        remote_kernel, 1, z.dtaps(1), [z.both, spec, spec], z.taps,
        [z.held(2, WIDTH), z.held(6, WIDTH), z.lines], 1,
    )(role, x, r_a, r_b)


def exact_parts(data):
    high = data.astype(BF16)
    rest = data - high.astype(F32)
    middle = rest.astype(BF16)
    return high, middle, (rest - middle.astype(F32)).astype(BF16)


def reverse_line(data, length, count):
    rows, width = data.shape
    total = length // WIDTH
    down = lax.broadcasted_iota(jnp.int32, (WIDTH, WIDTH), 0)
    across = lax.broadcasted_iota(jnp.int32, (WIDTH, WIDTH), 1)
    inner = jnp.where(down + across == WIDTH, 1.0, 0.0).astype(BF16)
    edge = jnp.where(down + across == 0, 1.0, 0.0).astype(BF16)
    zero = jnp.zeros((rows, WIDTH), F32)

    def block(t):
        return data[:, t * WIDTH : (t + 1) * WIDTH] if 0 <= t < width // WIDTH else zero

    done = []
    for j in range(count // WIDTH):
        found = zero
        for a, b in zip(exact_parts(block(total - 1 - j)), exact_parts(block(total - j))):
            found += dot(a, inner) + dot(b, edge)
        done.append(found)
    return jnp.concatenate(done, axis=1)


def arrange_kernel(role, mine, other, my_bias, other_bias, lead_taps, follow_taps, bias):
    groups, length = mine.shape

    def main(case):
        for part in (0, 1):
            taps = (mine if part == case else other)[...]
            ahead = jnp.concatenate([jnp.zeros((groups, WIDTH), F32), taps], axis=1)
            behind = reverse_line(taps, length, length + WIDTH)
            first, second = (ahead, behind) if case == 0 else (behind, ahead)
            lead_taps[part] = first
            follow_taps[part] = second
            line = (my_bias if part == case else other_bias)[...]
            bias[part] = jnp.broadcast_to(line, (WIDTH, line.shape[1])).T

    pick(role[0], main)


def natural(case, dtaps, count):
    if case == 0:
        return dtaps[:, WIDTH : WIDTH + count]
    return reverse_line(dtaps, dtaps.shape[1] - WIDTH, count)


def channel_line(dbias):
    square = dbias[...]
    if square.shape[0] < WIDTH:
        square = jnp.concatenate(
            [square, jnp.zeros((WIDTH - square.shape[0], WIDTH), F32)], axis=0
        )
    return jnp.sum(square.T, axis=0, keepdims=True)


def send_kernel(role, dtaps, dbias, sent):
    _, groups, width = dtaps.shape
    half = (width - WIDTH) // 2

    def main(case):
        sent[:, :half] = natural(case, dtaps[1 - case], half)
        sent[:, half:] = jnp.broadcast_to(channel_line(dbias.at[1 - case]), (groups, WIDTH))

    pick(role[0], main)


def receive_kernel(role, dtaps, dbias, far, came, grad_taps, grad_bias):
    length = dtaps.shape[2] - WIDTH
    half = length // 2

    def main(case):
        total = natural(case, dtaps[case] + far[0], length)
        grad_taps[:, :half] = total[:, :half] + came[:, :half]
        grad_taps[:, half:] = total[:, half:]
        grad_bias[...] = channel_line(dbias.at[case]) + came[0:1, half:]

    pick(role[0], main)


def whole_call(kernel, out_shape, *args):
    spec = lambda a: pl.BlockSpec(a.shape, lambda i, s: (0,) * len(a.shape))
    outs = out_shape if isinstance(out_shape, tuple) else (out_shape,)
    return pl.pallas_call(
        kernel,
        out_shape=out_shape,
        grid_spec=pltpu.PrefetchScalarGridSpec(
            num_scalar_prefetch=1,
            grid=(1,),
            in_specs=[spec(a) for a in args[1:]],
            out_specs=tuple(spec(o) for o in outs) if isinstance(out_shape, tuple) else spec(out_shape),
        ),
    )(*args)


def exchange(values):
    return lax.all_to_all(values, RING, split_axis=0, concat_axis=0)


def local(queries, key_stream, value_stream, filters, bias, grad_out):
    ranks = lax.axis_size(RING)
    role = lax.axis_index("half").astype(jnp.int32)[None]
    groups, length = filters.shape
    per = bias.shape[0]
    group = per // groups
    partner = [(i, (i + ranks) % (2 * ranks)) for i in range(2 * ranks)]
    swap = lambda a: lax.ppermute(a, ("half",) + RING, partner)

    bias = bias[None]
    other = swap(filters)
    other_bias = swap(bias)
    x = prepare(0, role, queries, key_stream, value_stream, grad_out, ranks)
    y = prepare(1, role, queries, key_stream, value_stream, grad_out, ranks)
    x = exchange(x)
    y = exchange(y)
    taps = jax.ShapeDtypeStruct((2, groups, length + WIDTH), F32)
    lead_taps, follow_taps, offsets = whole_call(
        arrange_kernel,
        (taps, taps, jax.ShapeDtypeStruct((2, per, WIDTH), F32)),
        role, filters, other, bias, other_bias,
    )
    r_a = swap(x[:, 0])
    r_b = swap(x[:, 1])
    one = lead(role, x, lead_taps, offsets, group)
    one = exchange(one)
    two, dtaps, dbias = local_part(role, x, y, follow_taps, offsets, group)
    half = jax.ShapeDtypeStruct((groups, length // 2 + WIDTH), F32)
    sent = whole_call(send_kernel, half, role, dtaps, dbias)
    came = swap(sent)
    two = cross_part(role, x, r_a, r_b, follow_taps, two, group)
    two = exchange(two)
    far = remote_part(role, x, r_a, r_b, follow_taps, group)
    grad_filters, grad_bias = whole_call(
        receive_kernel,
        (jax.ShapeDtypeStruct((groups, length), F32), jax.ShapeDtypeStruct((1, WIDTH), F32)),
        role, dtaps, dbias, far, came,
    )
    outs = finish(role, queries, key_stream, value_stream, grad_out, one, two, ranks)
    return (*outs, grad_filters, grad_bias[0, :per])


def solution(mesh):
    ctx, dp = mesh.devices.shape
    split = Mesh(mesh.devices.reshape(2, ctx // 2, dp), ("half", "ctx_low", "dp"))
    axes = ("half", "ctx_low", "dp")
    stream = P(None, axes)
    return jax.shard_map(
        local,
        mesh=split,
        in_specs=(stream, stream, stream, P(axes, None), P(axes), stream),
        out_specs=(stream, stream, stream, stream, P(axes, None), P(axes)),
        check_vma=False,
    )
```
